256 devices in a mesh: pair: 32 (over y, x, core), occ: 8 (over z).
Axes of the slice: x: 4, y: 4, z: 8, core: 2. Of those that a mesh axis runs over, the one named last changes fastest.
Arguments:
- half_ints: bfloat16 [8, 12288, 6144], P('occ', 'pair'), may hold values from -6 to 6
- pair_coef: bfloat16 [512, 12288], P('occ'), may hold values from -0.078125 to 0.078125
- mo_virtual: bfloat16 [5632, 6144], P('pair'), may hold values from -0.078125 to 0.078125
- screen: int32 [192], replicated, may hold values 0 or 1
- slot_block: int32 [192], replicated, may hold values from 0 to 191, each once
Outputs:
- mo_block: bfloat16 [5632, 8, 512], P('pair', 'occ')
The draws below stay inside these ranges and needn't reach their ends.
Inputs may be any that keep to these rules, and one draw needn't show every extreme that they name: `screen`: 1 where the pair block survives screening, 0 where it is dropped. `slot_block`: each logical pair block stands in exactly one storage slot; index k of pair holds slots k * 6 to k * 6 + 5.
All inputs are finite; a program needn't handle non-finite values.
Results may differ from the reference program's by a relative error of at most 0.0049.
Values may be sent and summed in bfloat16 or wider, within the bound.
No kernel may reach another device: no remote copies, remote signals or barrier semaphores. Data moves between devices by JAX's collectives and lax.ppermute only.
A program may use at most 128 MiB of HBM per device.

```python
import jax
import jax.numpy as jnp
from jax import lax

NB = 6144
NV = 5632
J = 512
BLK = 64
NPB = 192
NQ = 12288
I = 8


def with_ends(array, own_key, least, high):
    extent = array.shape
    spot = [jax.random.randint(jax.random.fold_in(own_key, axis), (), 0, extent[axis]) for axis in range(len(extent))]
    array = array.at[tuple(spot)].set(least)
    longest = extent.index(max(extent))
    spot[longest] = (spot[longest] + 1) % extent[longest]
    return array.at[tuple(spot)].set(high)


def block_levels(own_key, shape, shards, least, high):
    gain = 1.0
    for position, parts in shards:
        draws = jax.random.uniform(jax.random.fold_in(jax.random.fold_in(own_key, 6), position), (parts,), jnp.float32, least / len(shards), high / len(shards))
        gain = gain * jnp.repeat(jnp.exp(draws), shape[position] // parts).reshape((-1,) + (1,) * (len(shape) - 1 - position))
    return gain


def gaussian(own_key, dims, deviation, bound, split=(), held_as=jnp.bfloat16):
    entries = jax.random.normal(own_key, dims, jnp.float32) * deviation
    if len(split) > 0:
        entries = block_levels(own_key, dims, split, -0.22, 0.18) * entries
    return jnp.clip(entries, min=-bound, max=bound).astype(held_as)


def setup_inputs(seed: int = 0) -> dict:
    keys = jax.random.split(jax.random.key(seed), 6)
    return {
        "half_ints": gaussian(keys[0], (I, NQ, NB), 1.0, 6.0, ((0, 8), (1, 32))),
        "pair_coef": gaussian(keys[1], (J, NQ), (NQ // 2) ** -0.5, 0.078125, ((0, 8),)),
        "mo_virtual": gaussian(keys[2], (NV, NB), NB ** -0.5, 0.078125, ((0, 32),)),
        "screen": with_ends((jax.random.randint(keys[3], (NPB,), 0, 2) < 1).astype(jnp.int32), jax.random.fold_in(keys[3], 1), 0, 1),
        "slot_block": jax.random.permutation(keys[4], NPB).astype(jnp.int32),
    }


def reference(half_ints, pair_coef, mo_virtual, screen, slot_block):
    masked_coef = pair_coef.reshape(J, NPB, BLK) * screen.astype(jnp.bfloat16)[None, :, None]
    selected = jnp.take(masked_coef, slot_block.astype(jnp.int32), axis=1).reshape(J, NQ)

    def one_orbital(ints_row):
        occ_pair = jnp.dot(selected, ints_row, preferred_element_type=jnp.float32).astype(jnp.bfloat16)
        return jnp.dot(mo_virtual, occ_pair.T, preferred_element_type=jnp.float32).astype(jnp.bfloat16)

    stacked = lax.map(one_orbital, half_ints)
    return jnp.transpose(stacked, (1, 0, 2))
```

```python
import jax
import jax.numpy as jnp
from jax import lax
from jax.sharding import Mesh
from jax.sharding import PartitionSpec as P

Y, X, C, Z = 4, 4, 2, 8
SIZE = {"y": Y, "x": X, "core": C, "z": Z}


def shift(value, axis, step):
    size = SIZE[axis]
    return lax.ppermute(value, axis, [(i, (i + step) % size) for i in range(size)])


def rows(value, block, height):
    return lax.dynamic_slice_in_dim(value, block * height, height, 0)


def reduce_scatter(part, axis):
    size = SIZE[axis]
    height = part.shape[0] // size
    me = lax.axis_index(axis)
    got = []
    for step in range(1, size):
        out = rows(part, (me + step) % size, height).astype(jnp.bfloat16)
        got.append(shift(out, axis, step))
    total = rows(part, me, height)
    for piece in got:
        total = total + piece.astype(jnp.float32)
    return total


def gather(own, axis):
    size = SIZE[axis]
    height = own.shape[0]
    me = lax.axis_index(axis)
    whole = jnp.zeros((height * size, own.shape[1]), own.dtype)
    whole = lax.dynamic_update_slice_in_dim(whole, own, me * height, 0)
    for step in range(1, size):
        piece = shift(own, axis, step)
        whole = lax.dynamic_update_slice_in_dim(whole, piece, ((me - step) % size) * height, 0)
    return whole


def shards(half_ints, pair_coef, mo_virtual, screen, slot_block):
    core = lax.axis_index("core")
    own = (lax.axis_index("y") * X + lax.axis_index("x")) * C + core
    ints = half_ints[0]
    pairs, basis = ints.shape
    count = screen.shape[0]
    width = pair_coef.shape[1] // count
    held = pairs // width
    half = basis // 2

    blocks = lax.dynamic_slice_in_dim(slot_block, own * held, held, 0)
    picked = [
        lax.dynamic_slice_in_dim(pair_coef, blocks[s] * width, width, 1) * screen[blocks[s]].astype(jnp.bfloat16)
        for s in range(held)
    ]
    chosen = jnp.concatenate(picked, axis=1)
    mine = lax.all_gather(chosen, "z", axis=0, tiled=True)
    theirs = shift(mine, "core", 1)

    kept = lax.dynamic_slice_in_dim(ints, core * half, half, 1)
    given = lax.dynamic_slice_in_dim(ints, (1 - core) * half, half, 1)
    taken = shift(given, "core", 1)
    virt_kept = lax.dynamic_slice_in_dim(mo_virtual, core * half, half, 1)
    virt_given = lax.dynamic_slice_in_dim(mo_virtual, (1 - core) * half, half, 1)
    virt_taken = shift(virt_given, "core", 1)

    over = (((0,), (1,)), ((), ()))
    part = lax.dot_general(kept, mine, over, preferred_element_type=jnp.float32) + lax.dot_general(
        taken, theirs, over, preferred_element_type=jnp.float32
    )
    first, second = part[: half // 2], part[half // 2 :]
    first = reduce_scatter(reduce_scatter(first, "x"), "y").astype(jnp.bfloat16)
    second = reduce_scatter(reduce_scatter(second, "y"), "x").astype(jnp.bfloat16)
    first = gather(gather(first, "y"), "x")
    second = gather(gather(second, "x"), "y")

    quarter = half // 2
    def fold(virt):
        return jnp.dot(virt[:, :quarter], first, preferred_element_type=jnp.float32) + jnp.dot(
            virt[:, quarter:], second, preferred_element_type=jnp.float32
        )

    passed = shift(fold(virt_taken), "core", 1)
    out = (fold(virt_kept) + passed).astype(jnp.bfloat16)
    return out[:, None, :]


def solution(mesh):
    split = Mesh(mesh.devices.reshape(Y, X, C, Z), ("y", "x", "core", "z"))
    pair = ("y", "x", "core")
    placed = (P("z", pair, None), P("z", None), P(pair, None), P(), P())
    return jax.shard_map(
        shards, mesh=split, in_specs=placed, out_specs=P(pair, "z", None), check_vma=False
    )
```

```python
import jax
import jax.numpy as jnp
from jax import lax
from jax.experimental import pallas as pl
from jax.experimental.pallas import tpu as pltpu
from jax.sharding import Mesh
from jax.sharding import PartitionSpec as P

N, C, Z = 4, 2, 8
PAIR = ("y", "x", "core")
ORDER = (2, 1, 3)
F32, BF16 = jnp.float32, jnp.bfloat16


def after(value, *others):
    return lax.optimization_barrier((value, *others))[0]


def hop(value, leg, step):
    pairs = []
    for y in range(N):
        for x in range(N):
            for core in range(C):
                to_y, to_x = (y, (x + step) % N) if core == leg else ((y + step) % N, x)
                pairs.append(((y * N + x) * C + core, (to_y * N + to_x) * C + core))
    return lax.ppermute(value, PAIR, pairs)


def exchange(value, leg, mask):
    pairs = []
    for y in range(N):
        for x in range(N):
            for core in range(C):
                to_y, to_x = (y, x ^ mask) if core == leg else (y ^ mask, x)
                pairs.append(((y * N + x) * C + core, (to_y * N + to_x) * C + core))
    return lax.ppermute(value, PAIR, pairs)


def swap(value):
    return lax.ppermute(value, "core", [(0, 1), (1, 0)])


def layers(value, step):
    pairs = [(z, (z - step) % Z) for z in range(Z)] + [(Z + z, Z + (z + step) % Z) for z in range(Z)]
    return lax.ppermute(value, ("core", "z"), pairs)


def pick_columns(slots, screen, coef, width, first, second):
    rows = coef.shape[0]
    count = slots.shape[0] // (N * N * C)
    tile = 2 * width

    def kernel(place_ref, slots_ref, screen_ref, coef_ref, out):
        lane = lax.broadcasted_iota(jnp.int32, (rows, tile), 1)
        for p in range(count):
            halves = []
            for side in range(2):
                run, s = divmod(2 * p + side, count)
                block = slots_ref[place_ref[run] * count + s]
                at = pl.multiple_of(block // 2 * tile, tile)
                value = coef_ref[:, pl.ds(at, tile)].astype(F32) * screen_ref[block].astype(F32)
                halves.append(jnp.where(block % 2 != side, pltpu.roll(value, width, 1), value))
            out[:, p * tile : (p + 1) * tile] = jnp.where(lane < width, halves[0], halves[1]).astype(BF16)

    smem, vmem = pl.BlockSpec(memory_space=pltpu.SMEM), pl.BlockSpec(memory_space=pltpu.VMEM)
    return pl.pallas_call(
        kernel,
        out_shape=jax.ShapeDtypeStruct((rows, 2 * count * width), BF16),
        in_specs=[smem, smem, smem, vmem],
        out_specs=vmem,
        compiler_params=pltpu.CompilerParams(vmem_limit_bytes=20 << 20),
        name="pick",
    )(jnp.stack([first, second]).astype(jnp.int32), slots, screen, coef)


def turned(parts, places, height):
    whole = jnp.concatenate(parts, axis=0)
    rows = whole.shape[0]
    start = places % (rows // height) * height
    return lax.dynamic_slice_in_dim(jnp.concatenate([whole, whole], axis=0), start, rows, 0)


def gather_layers(own, core, z, *ready):
    rows, cols = own.shape
    next_one = layers(own, 1)
    next_two = layers(own, 2)
    pair = layers(after(jnp.concatenate([next_one, next_two], axis=0), *ready), 2)
    got = jnp.concatenate([next_one, next_two, pair], axis=0)
    other = swap(got)
    other = jnp.concatenate([other[:, cols // 2 :], other[:, : cols // 2]], axis=1)
    up, down = jnp.where(core == 0, got, other), jnp.where(core == 0, other, got)
    up, down = up.reshape(4, rows, cols), down.reshape(4, rows, cols)
    return turned([down[0], own, up[0], up[1], up[2], up[3], down[2], down[1]], 1 - z, rows)


def block_of(value, index, width, axis):
    return lax.dynamic_slice_in_dim(value, index * width, width, axis)


def add(parts):
    total = parts[0].astype(F32)
    for piece in parts[1:]:
        total = total + piece.astype(F32)
    return total


def shards(half_ints, pair_coef, mo_virtual, screen, slot_block):
    y, x, core, z = (lax.axis_index(a) for a in ("y", "x", "core", "z"))
    first, second = jnp.where(core == 0, x, y), jnp.where(core == 0, y, x)
    chip = y * N + x
    width = half_ints.shape[2] // (C * N)

    ints_taken = swap(half_ints)
    virt_taken = swap(mo_virtual)
    slot_width = pair_coef.shape[1] // screen.shape[0]
    own = pick_columns(slot_block, screen, pair_coef, slot_width, chip * C + core, chip * C + 1 - core)

    def ints_block(ints, step):
        return block_of(ints[0], N * core + (first + step) % N, width, 1)

    def virt_block(step):
        at = N * core + (first - step) % N
        return jnp.concatenate([block_of(mo_virtual, at, width, 1), block_of(virt_taken, at, width, 1)], axis=0)

    virt = [virt_block(0)] + [hop(virt_block(s), 0, N - s) for s in (1, 2, 3)]
    chosen = gather_layers(own, core, z, ints_taken)
    chosen = after(chosen, virt[1], virt[3])

    def product(step, chosen):
        both = jnp.concatenate([ints_block(half_ints, step), ints_block(ints_taken, step)], axis=0)
        return jnp.dot(chosen, both, preferred_element_type=F32)

    got = [hop(product(s, chosen).astype(BF16), 0, s) for s in ORDER]
    kept = lax.optimization_barrier(product(0, after(chosen, virt[2])))
    total = add([kept, *got])
    half = total.shape[0] // 2
    ends = [total[:half], total[half:]]
    for masks in ((1, 3), (3, 1)):
        ends = [part + exchange(part.astype(BF16), 1, mask).astype(F32) for part, mask in zip(ends, masks)]
    ends = [part.astype(BF16) for part in ends]
    summed = jnp.concatenate(ends, axis=0)

    def fold(step):
        return lax.dot_general(virt[step], summed, (((1,), (1,)), ((), ())), preferred_element_type=F32)

    got = [hop(fold(s).astype(BF16), 0, s) for s in ORDER]
    both = add([lax.optimization_barrier(fold(0)), *got])
    rows = mo_virtual.shape[0]
    out = (both[:rows] + swap(both[rows:])).astype(BF16)
    return out[:, None, :]


def solution(mesh):
    split = Mesh(mesh.devices.reshape(N, N, C, Z), ("y", "x", "core", "z"))
    placed = (P("z", PAIR, None), P("z", None), P(PAIR, None), P(), P())
    return jax.shard_map(
        shards, mesh=split, in_specs=placed, out_specs=P(PAIR, "z", None), check_vma=False
    )
```

```python
import jax
import jax.numpy as jnp
from jax import lax
from jax.experimental import pallas as pl
from jax.experimental.pallas import tpu as pltpu
from jax.sharding import Mesh
from jax.sharding import PartitionSpec as P

N, C, Z = 4, 2, 8
PAIR = ("y", "x", "core")
ORDER = (2, 1, 3)
F32, BF16 = jnp.float32, jnp.bfloat16


def after(value, *others):
    return lax.optimization_barrier((value, *others))[0]


def hop(value, leg, step):
    pairs = []
    for y in range(N):
        for x in range(N):
            for core in range(C):
                to_y, to_x = (y, (x + step) % N) if core == leg else ((y + step) % N, x)
                pairs.append(((y * N + x) * C + core, (to_y * N + to_x) * C + core))
    return lax.ppermute(value, PAIR, pairs)


def exchange(value, leg, mask):
    pairs = []
    for y in range(N):
        for x in range(N):
            for core in range(C):
                to_y, to_x = (y, x ^ mask) if core == leg else (y ^ mask, x)
                pairs.append(((y * N + x) * C + core, (to_y * N + to_x) * C + core))
    return lax.ppermute(value, PAIR, pairs)


def swap(value):
    return lax.ppermute(value, "core", [(0, 1), (1, 0)])


def layers(value, step):
    pairs = [(z, (z - step) % Z) for z in range(Z)] + [(Z + z, Z + (z + step) % Z) for z in range(Z)]
    return lax.ppermute(value, ("core", "z"), pairs)


def pick_columns(slots, screen, coef, width, first, second):
    rows = coef.shape[0]
    every = slots.shape[0]
    count = every // (N * N * C)
    tile = 2 * width

    def kernel(place_ref, table_ref, coef_ref, out):
        lane = lax.broadcasted_iota(jnp.int32, (rows, tile), 1)
        for p in range(count):
            halves = []
            for side in range(2):
                run, s = divmod(2 * p + side, count)
                block = table_ref[place_ref[run] * count + s]
                at = pl.multiple_of(block // 2 * tile, tile)
                value = coef_ref[:, pl.ds(at, tile)].astype(F32) * table_ref[every + block].astype(F32)
                halves.append(jnp.where(block % 2 != side, pltpu.roll(value, width, 1), value))
            out[:, p * tile : (p + 1) * tile] = jnp.where(lane < width, halves[0], halves[1]).astype(BF16)

    smem, vmem = pl.BlockSpec(memory_space=pltpu.SMEM), pl.BlockSpec(memory_space=pltpu.VMEM)
    return pl.pallas_call(
        kernel,
        out_shape=jax.ShapeDtypeStruct((rows, 2 * count * width), BF16),
        in_specs=[smem, smem, vmem],
        out_specs=vmem,
        compiler_params=pltpu.CompilerParams(vmem_limit_bytes=20 << 20),
        name="pick",
    )(jnp.stack([first, second]).astype(jnp.int32), jnp.concatenate([slots, screen]), coef)


def turned(parts, places, height):
    whole = jnp.concatenate(parts, axis=0)
    rows = whole.shape[0]
    start = places % (rows // height) * height
    return lax.dynamic_slice_in_dim(jnp.concatenate([whole, whole], axis=0), start, rows, 0)


def gather_layers(own, near, core, z, before):
    rows, cols = own.shape
    next_one, next_two = near
    sent, *before = lax.optimization_barrier((jnp.concatenate([next_one, next_two], axis=0), *before))
    pair = layers(sent, 2)
    got = jnp.concatenate([next_one, next_two, pair], axis=0)
    other = swap(got)
    other = jnp.concatenate([other[:, cols // 2 :], other[:, : cols // 2]], axis=1)
    up, down = jnp.where(core == 0, got, other), jnp.where(core == 0, other, got)
    up, down = up.reshape(4, rows, cols), down.reshape(4, rows, cols)
    return turned([down[0], own, up[0], up[1], up[2], up[3], down[2], down[1]], 1 - z, rows), before


def block_of(value, index, width, axis):
    return lax.dynamic_slice_in_dim(value, index * width, width, axis)


def add(parts):
    total = parts[0].astype(F32)
    for piece in parts[1:]:
        total = total + piece.astype(F32)
    return total


def shards(half_ints, pair_coef, mo_virtual, screen, slot_block):
    y, x, core, z = (lax.axis_index(a) for a in ("y", "x", "core", "z"))
    first, second = jnp.where(core == 0, x, y), jnp.where(core == 0, y, x)
    chip = y * N + x
    width = half_ints.shape[2] // (C * N)

    ints_taken = swap(half_ints)
    virt_taken = swap(mo_virtual)
    slot_width = pair_coef.shape[1] // screen.shape[0]
    own = pick_columns(slot_block, screen, pair_coef, slot_width, chip * C + core, chip * C + 1 - core)

    def ints_block(ints, step):
        return block_of(ints[0], N * core + (first + step) % N, width, 1)

    def virt_block(step):
        at = N * core + (first - step) % N
        return jnp.concatenate([block_of(mo_virtual, at, width, 1), block_of(virt_taken, at, width, 1)], axis=0)

    near = [layers(own, 1), layers(own, 2)]
    virt = [virt_block(0)] + [hop(virt_block(s), 0, N - s) for s in (1, 2, 3)]
    chosen, ints = gather_layers(own, near, core, z, (half_ints, ints_taken))

    def product(step, chosen):
        both = jnp.concatenate([ints_block(a, step) for a in ints], axis=0)
        return jnp.dot(chosen, both, preferred_element_type=F32)

    got = [hop(product(s, chosen).astype(BF16), 0, s) for s in ORDER]
    kept = lax.optimization_barrier(product(0, after(chosen, *virt[1:])))
    total = add([kept, *got])
    rows = total.shape[0] // 2
    ends = [total[:rows], total[rows:]]
    for masks in ((1, 3), (3, 1)):
        ends = [part + exchange(part.astype(BF16), 1, mask).astype(F32) for part, mask in zip(ends, masks)]
    ends = [part.astype(BF16) for part in ends]
    summed = jnp.concatenate(ends, axis=0)

    def fold(step):
        return lax.dot_general(virt[step], summed, (((1,), (1,)), ((), ())), preferred_element_type=F32)

    got = [hop(fold(s).astype(BF16), 0, s) for s in ORDER]
    both = add([lax.optimization_barrier(fold(0)), *got])
    rows = mo_virtual.shape[0]
    out = (both[:rows] + swap(both[rows:])).astype(BF16)
    return out[:, None, :]


def solution(mesh):
    split = Mesh(mesh.devices.reshape(N, N, C, Z), ("y", "x", "core", "z"))
    placed = (P("z", PAIR, None), P("z", None), P(PAIR, None), P(), P())
    return jax.shard_map(
        shards, mesh=split, in_specs=placed, out_specs=P(PAIR, "z", None), check_vma=False
    )
```

```python
import jax
import jax.numpy as jnp
from jax import lax
from jax.experimental import pallas as pl
from jax.experimental.pallas import tpu as pltpu
from jax.sharding import Mesh
from jax.sharding import PartitionSpec as P

N, C, Z = 4, 2, 8
PAIR = ("y", "x", "core")
ORDER = (2, 1, 3)
F32, BF16 = jnp.float32, jnp.bfloat16


def after(value, *others):
    return lax.optimization_barrier((value, *others))[0]


def hop(value, leg, step):
    pairs = []
    for y in range(N):
        for x in range(N):
            for core in range(C):
                to_y, to_x = (y, (x + step) % N) if core == leg else ((y + step) % N, x)
                pairs.append(((y * N + x) * C + core, (to_y * N + to_x) * C + core))
    return lax.ppermute(value, PAIR, pairs)


def exchange(value, leg, mask):
    pairs = []
    for y in range(N):
        for x in range(N):
            for core in range(C):
                to_y, to_x = (y, x ^ mask) if core == leg else (y ^ mask, x)
                pairs.append(((y * N + x) * C + core, (to_y * N + to_x) * C + core))
    return lax.ppermute(value, PAIR, pairs)


def swap(value):
    return lax.ppermute(value, "core", [(0, 1), (1, 0)])


def layers(value, step):
    pairs = [(z, (z - step) % Z) for z in range(Z)] + [(Z + z, Z + (z + step) % Z) for z in range(Z)]
    return lax.ppermute(value, ("core", "z"), pairs)


def pick_columns(slots, screen, coef, width, first, second):
    rows = coef.shape[0]
    every = slots.shape[0]
    count = every // (N * N * C)
    tile = 2 * width

    def kernel(place_ref, table_ref, coef_ref, out):
        lane = lax.broadcasted_iota(jnp.int32, (rows, tile), 1)
        for p in range(count):
            halves = []
            for side in range(2):
                run, s = divmod(2 * p + side, count)
                block = table_ref[place_ref[run] * count + s]
                at = pl.multiple_of(block // 2 * tile, tile)
                value = coef_ref[:, pl.ds(at, tile)].astype(F32) * table_ref[every + block].astype(F32)
                halves.append(jnp.where(block % 2 != side, pltpu.roll(value, width, 1), value))
            out[:, p * tile : (p + 1) * tile] = jnp.where(lane < width, halves[0], halves[1]).astype(BF16)

    smem, vmem = pl.BlockSpec(memory_space=pltpu.SMEM), pl.BlockSpec(memory_space=pltpu.VMEM)
    return pl.pallas_call(
        kernel,
        out_shape=jax.ShapeDtypeStruct((rows, 2 * count * width), BF16),
        in_specs=[smem, smem, vmem],
        out_specs=vmem,
        compiler_params=pltpu.CompilerParams(vmem_limit_bytes=20 << 20),
        name="pick",
    )(jnp.stack([first, second]).astype(jnp.int32), jnp.concatenate([slots, screen]), coef)


def turned(parts, places, height):
    whole = jnp.concatenate(parts, axis=0)
    rows = whole.shape[0]
    start = places % (rows // height) * height
    return lax.dynamic_slice_in_dim(jnp.concatenate([whole, whole], axis=0), start, rows, 0)


def gather_layers(own, near, core, z, before):
    rows, cols = own.shape
    next_one, next_two = near
    sent, *before = lax.optimization_barrier((jnp.concatenate([next_one, next_two], axis=0), *before))
    pair = layers(sent, 2)
    got = jnp.concatenate([next_one, next_two, pair], axis=0)
    other = swap(got)
    other = jnp.concatenate([other[:, cols // 2 :], other[:, : cols // 2]], axis=1)
    up, down = jnp.where(core == 0, got, other), jnp.where(core == 0, other, got)
    up, down = up.reshape(4, rows, cols), down.reshape(4, rows, cols)
    return turned([down[0], own, up[0], up[1], up[2], up[3], down[2], down[1]], 1 - z, rows), before


def block_of(value, index, width, axis):
    return lax.dynamic_slice_in_dim(value, index * width, width, axis)


def add(parts):
    total = parts[0].astype(F32)
    for piece in parts[1:]:
        total = total + piece.astype(F32)
    return total


def shards(half_ints, pair_coef, mo_virtual, screen, slot_block):
    y, x, core, z = (lax.axis_index(a) for a in ("y", "x", "core", "z"))
    first, second = jnp.where(core == 0, x, y), jnp.where(core == 0, y, x)
    chip = y * N + x
    width = half_ints.shape[2] // (C * N)

    ints_taken = swap(half_ints)
    virt_taken = swap(mo_virtual)
    slot_width = pair_coef.shape[1] // screen.shape[0]
    own = pick_columns(slot_block, screen, pair_coef, slot_width, chip * C + core, chip * C + 1 - core)

    def ints_block(ints, step):
        return block_of(ints[0], N * core + (first + step) % N, width, 1)

    def virt_block(step):
        at = N * core + (first - step) % N
        return jnp.concatenate([block_of(mo_virtual, at, width, 1), block_of(virt_taken, at, width, 1)], axis=0)

    near = [layers(own, 1), layers(own, 2)]
    virt = [virt_block(0)] + [hop(virt_block(s), 0, N - s) for s in (1, 2, 3)]
    chosen, ints = gather_layers(own, near, core, z, (half_ints, ints_taken))

    def product(step, chosen):
        both = jnp.concatenate([ints_block(a, step) for a in ints], axis=0)
        return jnp.dot(chosen, both, preferred_element_type=F32)

    got = [hop(product(s, chosen).astype(BF16), 0, s) for s in ORDER]
    kept = lax.optimization_barrier(product(0, after(chosen, *virt[1:])))
    total = add([kept, *got])
    rows = total.shape[0] // 2
    ends = [total[:rows], total[rows:]]
    for masks in ((1, 3), (3, 1)):
        ends = [part + exchange(part.astype(BF16), 1, mask).astype(F32) for part, mask in zip(ends, masks)]
    ends = [part.astype(BF16) for part in ends]
    summed = jnp.concatenate(ends, axis=0)

    height = mo_virtual.shape[0]

    def fold(rows):
        left = jnp.concatenate([virt[s][rows] for s in (*ORDER, 0)], axis=0)
        return lax.dot_general(left, summed, (((1,), (1,)), ((), ())), preferred_element_type=F32)

    whole = fold(slice(None))
    parts = {s: block_of(whole, k, C * height, 0) for k, s in enumerate((*ORDER, 0))}
    both = add([parts[0], *(hop(parts[s].astype(BF16), 0, s) for s in ORDER)])
    out = (both[:height] + swap(both[height:])).astype(BF16)
    return out[:, None, :]


def solution(mesh):
    split = Mesh(mesh.devices.reshape(N, N, C, Z), ("y", "x", "core", "z"))
    placed = (P("z", PAIR, None), P("z", None), P(PAIR, None), P(), P())
    return jax.shard_map(
        shards, mesh=split, in_specs=placed, out_specs=P(PAIR, "z", None), check_vma=False
    )
```
